32 devices in a mesh: grp: 2 (over y), wide: 16 (over z, x, core).
Axes of the slice: x: 2, y: 2, z: 4, core: 2. Of those that a mesh axis runs over, the one named last changes fastest.
Arguments:
- tokens: bfloat16 [32, 768, 384], P(('grp', 'wide')), parts along dimension 0, may hold values from -6 to 6
- row_gain: float32 [384], replicated, may hold values from 0.25 to 1.75
- row_qkv: bfloat16 [384, 1152], replicated, may hold values from -10 to 10
- row_out: bfloat16 [384, 384], replicated, may hold values from -0.3125 to 0.3125
- col_gain: float32 [384], replicated, may hold values from 0.25 to 1.75
- col_qkv: bfloat16 [384, 1152], replicated, may hold values from -10 to 10
- col_out: bfloat16 [384, 384], replicated, may hold values from -0.3125 to 0.3125
Outputs:
- result: bfloat16 [32, 768, 384], P(('grp', 'wide')), parts along dimension 0
The draws below stay inside these ranges and needn't reach their ends.
There are 2 independent parts, one for each index of `grp`. The reference program is written for one: setup_inputs(seed, part) draws one part's arguments, and reference() takes and returns one part's arrays. A program takes and returns all parts, laid end to end along the dimension named above; an argument that names none is the same for every part. Nothing has to cross between parts.
All inputs are finite; a program needn't handle non-finite values.
Results may differ from the reference program's by a relative error of at most 0.0075.
Values may be sent and summed in bfloat16 or wider, within the bound.
A program may use at most 64 MiB of HBM per device.

```python
import math
import jax
import jax.numpy as jnp
from jax import lax

C = 384
HEADS = 6
W = 768
H = 16


def draw_tokens(key, part):
    first_key = jax.random.fold_in(key, 11)
    values = jax.random.normal(first_key, (H, W, C), jnp.float32)
    return jnp.clip(values, -6.0, 6.0).astype(jnp.bfloat16)


def qkv_helper(key):
    base = jax.random.normal(jax.random.fold_in(key, 21), (C, 3 * C), jnp.float32) / math.sqrt(C)
    return jnp.clip(base, -10.0, 10.0).astype(jnp.bfloat16)


def draw_row_qkv(key, part):
    return qkv_helper(jax.random.fold_in(key, 31))


def draw_col_qkv(key, part):
    return qkv_helper(jax.random.fold_in(key, 32))


def bell_draw(own_key, extent, width, bound, kind=jnp.bfloat16):
    return jnp.clip(width * jax.random.normal(own_key, extent, jnp.float32), -bound, bound).astype(kind)


def setup_inputs(seed: int = 0, part: int = 0) -> dict:
    splits = jax.random.split(jax.random.key(seed), 8)
    part_keys = jax.random.split(jax.random.fold_in(splits[7], part), 8)
    return {
        "tokens": draw_tokens(jax.random.fold_in(jax.random.fold_in(splits[7], part), 71), part),
        "row_gain": jnp.clip(1.0 + 0.15 * jax.random.normal(splits[1], (C,), jnp.float32), 0.25, 1.75),
        "row_qkv": draw_row_qkv(jax.random.fold_in(splits[7], 71), part),
        "row_out": bell_draw(splits[3], (C, C), C ** -0.5, 0.3125),
        "col_gain": jnp.clip(1.0 + 0.15 * jax.random.normal(splits[4], (C,), jnp.float32), 0.25, 1.75),
        "col_qkv": draw_col_qkv(jax.random.fold_in(splits[7], 71), part),
        "col_out": bell_draw(splits[6], (C, C), C ** -0.5, 0.3125),
    }


def normalize(values, gain):
    floats = values.astype(jnp.float32)
    scale = lax.rsqrt(lax.optimization_barrier(jnp.mean(floats * floats, axis=-1, keepdims=True)) + 1e-06)
    return (floats * scale * gain).astype(jnp.bfloat16)

def attend(packed):
    channels = packed.shape[-1] // 3
    head_size = channels // HEADS
    shape = packed.shape[:2] + (HEADS, head_size)
    query = packed[..., :channels].reshape(shape).astype(jnp.float32)
    keys = packed[..., channels:2 * channels].reshape(shape).astype(jnp.float32)
    values = packed[..., 2 * channels:].reshape(shape).astype(jnp.float32)
    scores = jnp.einsum('qbhd,kbhd->bhqk', query, keys) * head_size ** (-0.5)
    scores = scores - lax.optimization_barrier(jnp.max(scores, axis=-1, keepdims=True))
    expo = jnp.exp(scores)
    weights = (expo / lax.optimization_barrier(jnp.sum(expo, axis=-1, keepdims=True))).astype(jnp.bfloat16)
    mixed = jnp.einsum('bhqk,kbhd->qbhd', weights.astype(jnp.float32), values)
    return mixed.reshape(packed.shape[:2] + (channels,)).astype(jnp.bfloat16)

def mix_rows(tokens, gain, qkv_weight, out_weight):
    rows, columns, channels = tokens.shape
    normed = normalize(tokens, gain).reshape(rows * columns, channels)
    packed = jnp.dot(normed, qkv_weight, preferred_element_type=jnp.float32).astype(jnp.bfloat16)
    packed = packed.reshape(rows, columns, 3 * channels)
    mixed = lax.map(lambda one_row: attend(one_row[:, None, :])[:, 0, :], packed)
    update = jnp.dot(mixed.reshape(rows * columns, channels), out_weight, preferred_element_type=jnp.float32)
    return (tokens.astype(jnp.float32) + update.reshape(tokens.shape)).astype(jnp.bfloat16)

def reference(tokens, row_gain, row_qkv, row_out, col_gain, col_qkv, col_out):
    first = mix_rows(tokens, row_gain, row_qkv, row_out)
    second = mix_rows(jnp.transpose(first, (1, 0, 2)), col_gain, col_qkv, col_out)
    return jnp.transpose(second, (1, 0, 2))
```

```python
import functools
import math

import jax
import jax.numpy as jnp
from jax import lax
from jax.experimental import pallas as pl
from jax.experimental.pallas import tpu as pltpu
from jax.sharding import PartitionSpec as P

HEADS = 6
AXIS = "wide"
TILE = 16
MESH = pl.DeviceIdType.MESH


def normalize(values, gain):
    floats = values.astype(jnp.float32)
    scale = lax.rsqrt(jnp.mean(floats * floats, axis=-1, keepdims=True) + 1e-06)
    return (floats * scale * gain).astype(jnp.bfloat16)


def attend(packed):
    channels = packed.shape[-1] // 3
    head_size = channels // HEADS
    shape = packed.shape[:2] + (HEADS, head_size)
    query = packed[..., :channels].reshape(shape)
    keys = packed[..., channels : 2 * channels].reshape(shape)
    values = packed[..., 2 * channels :].reshape(shape)
    scores = jnp.einsum(
        "qbhd,kbhd->bhqk", query, keys, preferred_element_type=jnp.float32
    ) * head_size ** (-0.5)
    scores = scores - jnp.max(scores, axis=-1, keepdims=True)
    expo = jnp.exp(scores)
    weights = (expo / jnp.sum(expo, axis=-1, keepdims=True)).astype(jnp.bfloat16)
    mixed = jnp.einsum("bhqk,kbhd->qbhd", weights, values, preferred_element_type=jnp.float32)
    return mixed.reshape(packed.shape[:2] + (channels,)).astype(jnp.bfloat16)


def project(flat, weight):
    return jnp.dot(flat, weight, preferred_element_type=jnp.float32).astype(jnp.bfloat16)


def residual_add(base, mixed, weight):
    rows, columns, channels = base.shape
    update = jnp.dot(
        mixed.reshape(rows * columns, channels), weight, preferred_element_type=jnp.float32
    )
    return (base.astype(jnp.float32) + update.reshape(base.shape)).astype(jnp.bfloat16)


def plain(tokens, row_gain, row_qkv, row_out, col_gain, col_qkv, col_out):
    rows, columns, channels = tokens.shape
    normed = normalize(tokens, row_gain).reshape(rows * columns, channels)
    packed = project(normed, row_qkv).reshape(rows, columns, 3 * channels)
    mixed = lax.map(lambda one_row: attend(one_row[:, None, :])[:, 0, :], packed)
    first = residual_add(tokens, mixed, row_out)
    moved = lax.all_to_all(first, AXIS, split_axis=1, concat_axis=0, tiled=True)
    length, count, _ = moved.shape
    flat = normalize(moved, col_gain).reshape(length * count, channels)
    column_mixed = attend(project(flat, col_qkv).reshape(length, count, 3 * channels))
    returned = lax.all_to_all(column_mixed, AXIS, split_axis=0, concat_axis=1, tiled=True)
    return residual_add(first, returned, col_out)


def kernel(
    x_hbm, rg_hbm, rqkv_hbm, rout_hbm, cg_hbm, cqkv_hbm, cout_hbm,
    out_ref,
    rg_ref, cg_ref, x_ref, rkv_ref, rq_ref, rout_ref, cqkv_ref, cout_ref,
    n_ref, k_ref, v_ref, cv_ref, send_ref, recv_ref, back_ref,
    load_sem, sent_sem, r1_sem, r2_sem,
):
    n, _, channels = x_hbm.shape
    chunks = x_ref.shape[0]
    size = n * TILE
    half = n // 2
    head = channels // HEADS
    per = 128 // head
    pairs = channels // 128
    me = lax.axis_index(AXIS)
    mine = me // half
    other = 1 - mine

    loads = [
        pltpu.make_async_copy(
            x_hbm.at[:, pl.ds(c * TILE, TILE), :], x_ref.at[c], load_sem.at[c]
        )
        for c in range(chunks)
    ]
    weights = [
        pltpu.make_async_copy(src, dst, load_sem.at[chunks + i])
        for i, (src, dst) in enumerate(
            [
                (rg_hbm, rg_ref.at[0]),
                (rqkv_hbm.at[:, pl.ds(channels, 2 * channels)], rkv_ref),
                (rqkv_hbm.at[:, pl.ds(0, channels)], rq_ref),
                (rout_hbm, rout_ref),
                (cg_hbm, cg_ref.at[0]),
                (cqkv_hbm, cqkv_ref),
                (cout_hbm, cout_ref),
            ]
        )
    ]
    for copy in [loads[0]] + weights[:2] + loads[1:] + weights[2:4]:
        copy.start()

    barrier = pltpu.get_barrier_semaphore()

    def greet(j, carry):
        peer = lax.rem(me + j, n)
        pl.semaphore_signal(barrier, inc=1, device_id={AXIS: peer}, device_id_type=MESH)
        return carry

    lax.fori_loop(1, n, greet, 0)

    factor = head ** (-0.5) * math.log2(math.e)
    ones = jnp.ones((size, 128), jnp.bfloat16)

    def attention(query, keys, values, mask):
        mixed = None
        lane = lax.broadcasted_iota(jnp.int32, query.shape, 1)
        for h in range(per):
            part = (lane >= h * head) & (lane < (h + 1) * head)
            one = jnp.where(part, query, jnp.zeros_like(query))
            scores = lax.dot_general(
                one, keys, (((1,), (1,)), ((), ())), preferred_element_type=jnp.float32
            )
            if mask is not None:
                scores = jnp.where(mask, scores, -jnp.inf)
            peak = jnp.max(scores, axis=-1, keepdims=True)
            expo = jnp.exp2(scores - peak).astype(jnp.bfloat16)
            both = jnp.dot(expo, values, preferred_element_type=jnp.float32)
            own = both[:, :128] / both[:, 128:]
            mixed = own if mixed is None else jnp.where(part, own, mixed)
        return mixed.astype(jnp.bfloat16)

    for copy in loads + weights[:2]:
        copy.wait()
    for c in range(chunks):
        normed = normalize(x_ref[c].reshape(size, channels), rg_ref[...])
        n_ref[c] = normed.reshape(n, TILE, channels)
        packed = jnp.dot(normed, rkv_ref[...], preferred_element_type=jnp.float32)
        k_ref[pl.ds(c * size, size), :] = packed[:, :channels].astype(jnp.bfloat16)
        for p in range(pairs):
            at = channels + p * 128
            v_ref[p, pl.ds(c * size, size), :128] = packed[:, at : at + 128].astype(jnp.bfloat16)
            v_ref[p, pl.ds(c * size, size), 128:] = ones
    for p in range(pairs):
        cv_ref[p, :, 128:] = ones
    for copy in weights[4:]:
        copy.start()
    weights[2].wait()
    weights[3].wait()

    def copy_out(c, peer):
        return pltpu.make_async_remote_copy(
            src_ref=send_ref.at[c, peer], dst_ref=recv_ref.at[c, me],
            send_sem=sent_sem, recv_sem=r1_sem.at[c],
            device_id={AXIS: peer}, device_id_type=MESH,
        )

    def copies_in(c):
        whole = recv_ref.at[c, pl.ds(0, n - 1)]
        return pltpu.make_async_copy(whole, whole, r1_sem.at[c])

    def back_out(c, peer):
        return pltpu.make_async_remote_copy(
            src_ref=back_ref.at[c, peer], dst_ref=out_ref.at[me, pl.ds(c * TILE, TILE), :],
            send_sem=sent_sem, recv_sem=r2_sem,
            device_id={AXIS: peer}, device_id_type=MESH,
        )

    def across(body, lo=0, hi=half):
        def step(j, carry):
            body(other * half + j)
            return carry

        lax.fori_loop(lo, hi, step, 0)

    def along(body):
        def step(j, carry):
            body(mine * half + lax.rem(me + j, half))
            return carry

        lax.fori_loop(1, half, step, 0)

    def peers(body):
        across(body)
        along(body)

    def row_unit(c, start, count):
        at = pl.ds(start, count)
        normed = n_ref[c, at].reshape(count * TILE, channels)
        query = jnp.dot(normed, rq_ref[...], preferred_element_type=jnp.float32)
        query = (query * factor).astype(jnp.bfloat16)
        mixed = jnp.concatenate(
            [
                attention(
                    query[:, p * 128 : (p + 1) * 128],
                    k_ref[:, p * 128 : (p + 1) * 128],
                    v_ref[p],
                    None,
                )
                for p in range(pairs)
            ],
            axis=1,
        )
        update = jnp.dot(mixed, rout_ref[...], preferred_element_type=jnp.float32)
        base = x_ref[c, at].reshape(count * TILE, channels).astype(jnp.float32)
        first = (base + update).astype(jnp.bfloat16)
        send_ref[c, at] = first.reshape(count, TILE, channels)

    def row_across(c, splits=1):
        count = half // splits
        for i in range(splits):
            row_unit(c, other * half + i * count, count)
            if i == 0 and splits > 1:
                pl.semaphore_wait(barrier, n - 1)
            across(lambda peer: copy_out(c, peer).start(), i * count, (i + 1) * count)

    def row_along(c):
        row_unit(c, mine * half, half)
        along(lambda peer: copy_out(c, peer).start())
        recv_ref[c, me] = send_ref[c, me]

    def row_step(c, carry):
        row_across(c)
        row_along(c - 1)
        return carry

    row_across(0, 2)
    lax.fori_loop(1, chunks, row_step, 0)
    row_along(chunks - 1)
    for copy in weights[4:]:
        copy.wait()

    at_row = lax.broadcasted_iota(jnp.int32, (size, size), 0)
    at_col = lax.broadcasted_iota(jnp.int32, (size, size), 1)
    same = lax.rem(at_row, TILE) == lax.rem(at_col, TILE)

    def col_chunk(c, carry):
        copies_in(c).wait()
        base = recv_ref[c].reshape(size, channels)
        normed = normalize(base, cg_ref[...])
        packed = jnp.dot(normed, cqkv_ref[...], preferred_element_type=jnp.float32)
        query = (packed[:, :channels] * factor).astype(jnp.bfloat16)
        keys = packed[:, channels : 2 * channels].astype(jnp.bfloat16)
        for p in range(pairs):
            at = 2 * channels + p * 128
            cv_ref[p, :, :128] = packed[:, at : at + 128].astype(jnp.bfloat16)
        mixed = jnp.concatenate(
            [
                attention(
                    query[:, p * 128 : (p + 1) * 128],
                    keys[:, p * 128 : (p + 1) * 128],
                    cv_ref[p],
                    same,
                )
                for p in range(pairs)
            ],
            axis=1,
        )
        update = jnp.dot(mixed, cout_ref[...], preferred_element_type=jnp.float32)
        result = (base.astype(jnp.float32) + update).astype(jnp.bfloat16)
        back_ref[c] = result.reshape(n, TILE, channels)
        peers(lambda peer: back_out(c, peer).start())
        out_ref[me, pl.ds(c * TILE, TILE), :] = back_ref[c, me]
        return carry

    lax.fori_loop(0, chunks, col_chunk, 0)

    out_part = out_ref.at[pl.ds(0, n - 1)]
    send_part = send_ref.at[:, pl.ds(0, n - 1)]
    back_part = back_ref.at[:, pl.ds(0, n - 1)]
    pltpu.make_async_copy(send_part, send_part, sent_sem).wait()
    pltpu.make_async_copy(back_part, back_part, sent_sem).wait()
    pltpu.make_async_copy(out_part, out_part, r2_sem).wait()


def fused(n, tokens, row_gain, row_qkv, row_out, col_gain, col_qkv, col_out):
    _, columns, channels = tokens.shape
    chunks = columns // (n * TILE)
    size = n * TILE
    pairs = channels // 128
    bf16 = jnp.bfloat16
    hbm = pl.BlockSpec(memory_space=pl.ANY)
    dma = pltpu.SemaphoreType.DMA
    flops = 2 * columns * channels * (8 * channels + 2 * columns + 2 * size)
    out = pl.pallas_call(
        kernel,
        out_shape=pltpu.VMEM((n, columns // n, channels), bf16),
        in_specs=[hbm] * 7,
        out_specs=pl.BlockSpec(memory_space=pltpu.VMEM),
        scratch_shapes=[
            pltpu.VMEM((1, channels), jnp.float32),
            pltpu.VMEM((1, channels), jnp.float32),
            pltpu.VMEM((chunks, n, TILE, channels), bf16),
            pltpu.VMEM((channels, 2 * channels), bf16),
            pltpu.VMEM((channels, channels), bf16),
            pltpu.VMEM((channels, channels), bf16),
            pltpu.VMEM((channels, 3 * channels), bf16),
            pltpu.VMEM((channels, channels), bf16),
            pltpu.VMEM((chunks, n, TILE, channels), bf16),
            pltpu.VMEM((columns, channels), bf16),
            pltpu.VMEM((pairs, columns, 256), bf16),
            pltpu.VMEM((pairs, size, 256), bf16),
            pltpu.VMEM((chunks, n, TILE, channels), bf16),
            pltpu.VMEM((chunks, n, TILE, channels), bf16),
            pltpu.VMEM((chunks, n, TILE, channels), bf16),
            dma((chunks + 7,)),
            dma(()),
            dma((chunks,)),
            dma(()),
        ],
        compiler_params=pltpu.CompilerParams(
            collective_id=0, has_side_effects=True, vmem_limit_bytes=60000000
        ),
        cost_estimate=pl.CostEstimate(
            flops=flops, bytes_accessed=8 * columns * channels, transcendentals=0
        ),
    )(
        tokens.reshape(n, columns // n, channels),
        row_gain,
        row_qkv,
        row_out,
        col_gain,
        col_qkv,
        col_out,
    )
    return out.reshape(tokens.shape)


def solution(mesh):
    n = mesh.shape[AXIS]

    def body(tokens, *rest):
        rows, columns, channels = tokens.shape
        whole_tiles = rows == 1 and columns % (n * TILE) == 0 and channels % 128 == 0
        if n % 4 == 0 and whole_tiles and 128 % (channels // HEADS) == 0:
            return fused(n, tokens, *rest)
        return plain(tokens, *rest)

    in_specs = (P(("grp", AXIS), None, None), P(), P(), P(), P(), P(), P())
    out_specs = P(("grp", AXIS), None, None)
    return jax.shard_map(body, mesh=mesh, in_specs=in_specs, out_specs=out_specs, check_vma=False)
```

```python
import functools
import math

import jax
import jax.numpy as jnp
from jax import lax
from jax.experimental import pallas as pl
from jax.experimental.pallas import tpu as pltpu
from jax.sharding import PartitionSpec as P

HEADS = 6
AXIS = "wide"
TILE = 16
MESH = pl.DeviceIdType.MESH


def normalize(values, gain):
    floats = values.astype(jnp.float32)
    scale = lax.rsqrt(jnp.mean(floats * floats, axis=-1, keepdims=True) + 1e-06)
    return (floats * scale * gain).astype(jnp.bfloat16)


def attend(packed):
    channels = packed.shape[-1] // 3
    head_size = channels // HEADS
    shape = packed.shape[:2] + (HEADS, head_size)
    query = packed[..., :channels].reshape(shape)
    keys = packed[..., channels : 2 * channels].reshape(shape)
    values = packed[..., 2 * channels :].reshape(shape)
    scores = jnp.einsum(
        "qbhd,kbhd->bhqk", query, keys, preferred_element_type=jnp.float32
    ) * head_size ** (-0.5)
    scores = scores - jnp.max(scores, axis=-1, keepdims=True)
    expo = jnp.exp(scores)
    weights = (expo / jnp.sum(expo, axis=-1, keepdims=True)).astype(jnp.bfloat16)
    mixed = jnp.einsum("bhqk,kbhd->qbhd", weights, values, preferred_element_type=jnp.float32)
    return mixed.reshape(packed.shape[:2] + (channels,)).astype(jnp.bfloat16)


def project(flat, weight):
    return jnp.dot(flat, weight, preferred_element_type=jnp.float32).astype(jnp.bfloat16)


def residual_add(base, mixed, weight):
    rows, columns, channels = base.shape
    update = jnp.dot(
        mixed.reshape(rows * columns, channels), weight, preferred_element_type=jnp.float32
    )
    return (base.astype(jnp.float32) + update.reshape(base.shape)).astype(jnp.bfloat16)


def plain(tokens, row_gain, row_qkv, row_out, col_gain, col_qkv, col_out):
    rows, columns, channels = tokens.shape
    normed = normalize(tokens, row_gain).reshape(rows * columns, channels)
    packed = project(normed, row_qkv).reshape(rows, columns, 3 * channels)
    mixed = lax.map(lambda one_row: attend(one_row[:, None, :])[:, 0, :], packed)
    first = residual_add(tokens, mixed, row_out)
    moved = lax.all_to_all(first, AXIS, split_axis=1, concat_axis=0, tiled=True)
    length, count, _ = moved.shape
    flat = normalize(moved, col_gain).reshape(length * count, channels)
    column_mixed = attend(project(flat, col_qkv).reshape(length, count, 3 * channels))
    returned = lax.all_to_all(column_mixed, AXIS, split_axis=0, concat_axis=1, tiled=True)
    return residual_add(first, returned, col_out)


def kernel(
    x_hbm, rg_hbm, rqkv_hbm, rout_hbm, cg_hbm, cqkv_hbm, cout_hbm,
    out_ref,
    rg_ref, cg_ref, x_ref, rkv_ref, rq_ref, rout_ref, cqkv_ref, cout_ref,
    n_ref, k_ref, v_ref, cv_ref, send_ref, recv_ref, back_ref,
    load_sem, sent_sem, r1_sem, r2_sem,
):
    n, _, channels = x_hbm.shape
    chunks = x_ref.shape[0]
    size = n * TILE
    half = n // 2
    early = 2
    head = channels // HEADS
    per = 128 // head
    pairs = channels // 128
    me = lax.axis_index(AXIS)
    mine = me // half
    other = 1 - mine

    loads = [
        pltpu.make_async_copy(
            x_hbm.at[:, pl.ds(c * TILE, TILE), :], x_ref.at[c], load_sem.at[c]
        )
        for c in range(chunks)
    ]
    weights = [
        pltpu.make_async_copy(src, dst, load_sem.at[chunks + i])
        for i, (src, dst) in enumerate(
            [
                (rg_hbm, rg_ref.at[0]),
                (rqkv_hbm.at[:, pl.ds(channels, 2 * channels)], rkv_ref),
                (rqkv_hbm.at[:, pl.ds(0, channels)], rq_ref),
                (rout_hbm, rout_ref),
                (cg_hbm, cg_ref.at[0]),
                (cqkv_hbm, cqkv_ref),
                (cout_hbm, cout_ref),
            ]
        )
    ]
    for copy in weights[:1] + loads + weights[1:4]:
        copy.start()

    barrier = pltpu.get_barrier_semaphore()

    def greet(j, carry):
        peer = lax.rem(me + j, n)
        pl.semaphore_signal(barrier, inc=1, device_id={AXIS: peer}, device_id_type=MESH)
        return carry

    lax.fori_loop(1, n, greet, 0)

    factor = head ** (-0.5) * math.log2(math.e)
    ones = jnp.ones((size, 128), jnp.bfloat16)

    def attention(query, keys, values, mask):
        count = query.shape[0]
        lane = lax.broadcasted_iota(jnp.int32, query.shape, 1) // head
        apart = jnp.concatenate(
            [jnp.where(lane == h, query, jnp.zeros_like(query)) for h in range(per)], axis=0
        )
        scores = lax.dot_general(
            apart, keys, (((1,), (1,)), ((), ())), preferred_element_type=jnp.float32
        )
        if mask is not None:
            scores = jnp.where(mask, scores, -jnp.inf)
        peak = jnp.max(scores, axis=-1, keepdims=True)
        expo = jnp.exp2(scores - peak).astype(jnp.bfloat16)
        both = jnp.dot(expo, values, preferred_element_type=jnp.float32)
        both = both[:, :128] / both[:, 128:]
        mixed = both[:count]
        for h in range(1, per):
            mixed = jnp.where(lane == h, both[h * count : (h + 1) * count], mixed)
        return mixed.astype(jnp.bfloat16)

    for copy in loads + weights[:1]:
        copy.wait()
    for c in range(chunks):
        normed = normalize(x_ref[c].reshape(size, channels), rg_ref[...])
        n_ref[c] = normed.reshape(n, TILE, channels)
    weights[1].wait()
    for c in range(chunks):
        normed = n_ref[c].reshape(size, channels)
        packed = jnp.dot(normed, rkv_ref[...], preferred_element_type=jnp.float32)
        k_ref[pl.ds(c * size, size), :] = packed[:, :channels].astype(jnp.bfloat16)
        for p in range(pairs):
            at = channels + p * 128
            v_ref[p, pl.ds(c * size, size), :128] = packed[:, at : at + 128].astype(jnp.bfloat16)
            v_ref[p, pl.ds(c * size, size), 128:] = ones
    for p in range(pairs):
        cv_ref[p, :, 128:] = ones
    for copy in weights[4:]:
        copy.start()
    weights[2].wait()
    weights[3].wait()

    def copy_out(c, peer):
        return pltpu.make_async_remote_copy(
            src_ref=send_ref.at[c, peer], dst_ref=recv_ref.at[c, me],
            send_sem=sent_sem, recv_sem=r1_sem.at[c],
            device_id={AXIS: peer}, device_id_type=MESH,
        )

    def copies_in(c):
        whole = recv_ref.at[c, pl.ds(0, n - 1)]
        return pltpu.make_async_copy(whole, whole, r1_sem.at[c])

    def back_out(c, peer):
        return pltpu.make_async_remote_copy(
            src_ref=back_ref.at[c, peer], dst_ref=out_ref.at[me, pl.ds(c * TILE, TILE), :],
            send_sem=sent_sem, recv_sem=r2_sem,
            device_id={AXIS: peer}, device_id_type=MESH,
        )

    def across(body, lo=0, hi=half):
        def step(j, carry):
            body(other * half + j)
            return carry

        lax.fori_loop(lo, hi, step, 0)

    def along(body):
        def step(j, carry):
            body(mine * half + lax.rem(me + j, half))
            return carry

        lax.fori_loop(1, half, step, 0)

    def send_back(c, lo, hi):
        def skip(j):
            return mine * half + j + jnp.where(j >= me - mine * half, 1, 0)

        def step(k, carry):
            lower = jnp.where(k < half, k, skip(k - half))
            upper = jnp.where(k < half + early, half + lax.rem((k - early) * (half // 2) + (k - early) // 2, half), skip(k - half))
            upper = jnp.where(k < early, skip(k), upper)
            back_out(c, jnp.where(mine == 1, lower, upper)).start()
            return carry

        lax.fori_loop(lo, hi, step, 0)

    def row_unit(c, start, count):
        at = pl.ds(start, count)
        normed = n_ref[c, at].reshape(count * TILE, channels)
        query = jnp.dot(normed, rq_ref[...], preferred_element_type=jnp.float32)
        query = (query * factor).astype(jnp.bfloat16)
        mixed = jnp.concatenate(
            [
                attention(
                    query[:, p * 128 : (p + 1) * 128],
                    k_ref[:, p * 128 : (p + 1) * 128],
                    v_ref[p],
                    None,
                )
                for p in range(pairs)
            ],
            axis=1,
        )
        update = jnp.dot(mixed, rout_ref[...], preferred_element_type=jnp.float32)
        base = x_ref[c, at].reshape(count * TILE, channels).astype(jnp.float32)
        first = (base + update).astype(jnp.bfloat16)
        send_ref[c, at] = first.reshape(count, TILE, channels)

    def row_across(c, splits=1):
        count = half // splits
        for i in range(splits):
            row_unit(c, other * half + i * count, count)
            if i == 0 and splits > 1:
                pl.semaphore_wait(barrier, n - 1)
            across(lambda peer: copy_out(c, peer).start(), i * count, (i + 1) * count)

    def row_along(c):
        row_unit(c, mine * half, half)
        along(lambda peer: copy_out(c, peer).start())
        recv_ref[c, me] = send_ref[c, me]

    def row_step(c, carry):
        row_across(c)
        row_along(c - 1)
        return carry

    row_across(0, 2)
    lax.fori_loop(1, chunks, row_step, 0)
    row_along(chunks - 1)
    for copy in weights[4:]:
        copy.wait()

    at_row = lax.broadcasted_iota(jnp.int32, (per * size, size), 0)
    at_col = lax.broadcasted_iota(jnp.int32, (per * size, size), 1)
    same = lax.rem(at_row, TILE) == lax.rem(at_col, TILE)

    def col_chunk(c, carry):
        copies_in(c).wait()
        base = recv_ref[c].reshape(size, channels)
        normed = normalize(base, cg_ref[...])
        packed = jnp.dot(normed, cqkv_ref[...], preferred_element_type=jnp.float32)
        query = (packed[:, :channels] * factor).astype(jnp.bfloat16)
        keys = packed[:, channels : 2 * channels].astype(jnp.bfloat16)
        for p in range(pairs):
            at = 2 * channels + p * 128
            cv_ref[p, :, :128] = packed[:, at : at + 128].astype(jnp.bfloat16)
        mixed = jnp.concatenate(
            [
                attention(
                    query[:, p * 128 : (p + 1) * 128],
                    keys[:, p * 128 : (p + 1) * 128],
                    cv_ref[p],
                    same,
                )
                for p in range(pairs)
            ],
            axis=1,
        )
        update = jnp.dot(mixed, cout_ref[...], preferred_element_type=jnp.float32)
        result = (base.astype(jnp.float32) + update).astype(jnp.bfloat16)
        back_ref[c] = result.reshape(n, TILE, channels)

        @pl.when(c < chunks - 2)
        def _():
            send_back(c, 0, n - 1)

        out_ref[me, pl.ds(c * TILE, TILE), :] = back_ref[c, me]
        return carry

    lax.fori_loop(0, chunks, col_chunk, 0)
    for lo, hi in [(0, early), (early, n - 1)]:
        for c in range(max(chunks - 2, 0), chunks):
            send_back(c, lo, hi)

    out_part = out_ref.at[pl.ds(0, n - 1)]
    send_part = send_ref.at[:, pl.ds(0, n - 1)]
    back_part = back_ref.at[:, pl.ds(0, n - 1)]
    pltpu.make_async_copy(send_part, send_part, sent_sem).wait()
    pltpu.make_async_copy(back_part, back_part, sent_sem).wait()
    pltpu.make_async_copy(out_part, out_part, r2_sem).wait()


def fused(n, tokens, row_gain, row_qkv, row_out, col_gain, col_qkv, col_out):
    _, columns, channels = tokens.shape
    chunks = columns // (n * TILE)
    size = n * TILE
    pairs = channels // 128
    bf16 = jnp.bfloat16
    hbm = pl.BlockSpec(memory_space=pl.ANY)
    dma = pltpu.SemaphoreType.DMA
    flops = 2 * columns * channels * (8 * channels + 2 * columns + 2 * size)
    out = pl.pallas_call(
        kernel,
        out_shape=pltpu.VMEM((n, columns // n, channels), bf16),
        in_specs=[hbm] * 7,
        out_specs=pl.BlockSpec(memory_space=pltpu.VMEM),
        scratch_shapes=[
            pltpu.VMEM((1, channels), jnp.float32),
            pltpu.VMEM((1, channels), jnp.float32),
            pltpu.VMEM((chunks, n, TILE, channels), bf16),
            pltpu.VMEM((channels, 2 * channels), bf16),
            pltpu.VMEM((channels, channels), bf16),
            pltpu.VMEM((channels, channels), bf16),
            pltpu.VMEM((channels, 3 * channels), bf16),
            pltpu.VMEM((channels, channels), bf16),
            pltpu.VMEM((chunks, n, TILE, channels), bf16),
            pltpu.VMEM((columns, channels), bf16),
            pltpu.VMEM((pairs, columns, 256), bf16),
            pltpu.VMEM((pairs, size, 256), bf16),
            pltpu.VMEM((chunks, n, TILE, channels), bf16),
            pltpu.VMEM((chunks, n, TILE, channels), bf16),
            pltpu.VMEM((chunks, n, TILE, channels), bf16),
            dma((chunks + 7,)),
            dma(()),
            dma((chunks,)),
            dma(()),
        ],
        compiler_params=pltpu.CompilerParams(
            collective_id=0, has_side_effects=True, vmem_limit_bytes=60000000
        ),
        cost_estimate=pl.CostEstimate(
            flops=flops, bytes_accessed=8 * columns * channels, transcendentals=0
        ),
    )(
        tokens.reshape(n, columns // n, channels),
        row_gain,
        row_qkv,
        row_out,
        col_gain,
        col_qkv,
        col_out,
    )
    return out.reshape(tokens.shape)


def solution(mesh):
    n = mesh.shape[AXIS]

    def body(tokens, *rest):
        rows, columns, channels = tokens.shape
        whole_tiles = rows == 1 and columns % (n * TILE) == 0 and channels % 128 == 0
        if n % 4 == 0 and whole_tiles and 128 % (channels // HEADS) == 0:
            return fused(n, tokens, *rest)
        return plain(tokens, *rest)

    in_specs = (P(("grp", AXIS), None, None), P(), P(), P(), P(), P(), P())
    out_specs = P(("grp", AXIS), None, None)
    return jax.shard_map(body, mesh=mesh, in_specs=in_specs, out_specs=out_specs, check_vma=False)
```

```python
import functools
import math

import jax
import jax.numpy as jnp
from jax import lax
from jax.experimental import pallas as pl
from jax.experimental.pallas import tpu as pltpu
from jax.sharding import PartitionSpec as P

HEADS = 6
AXIS = "wide"
TILE = 16
MESH = pl.DeviceIdType.MESH


def normalize(values, gain):
    floats = values.astype(jnp.float32)
    scale = lax.rsqrt(jnp.mean(floats * floats, axis=-1, keepdims=True) + 1e-06)
    return (floats * scale * gain).astype(jnp.bfloat16)


def attend(packed):
    channels = packed.shape[-1] // 3
    head_size = channels // HEADS
    shape = packed.shape[:2] + (HEADS, head_size)
    query = packed[..., :channels].reshape(shape)
    keys = packed[..., channels : 2 * channels].reshape(shape)
    values = packed[..., 2 * channels :].reshape(shape)
    scores = jnp.einsum(
        "qbhd,kbhd->bhqk", query, keys, preferred_element_type=jnp.float32
    ) * head_size ** (-0.5)
    scores = scores - jnp.max(scores, axis=-1, keepdims=True)
    expo = jnp.exp(scores)
    weights = (expo / jnp.sum(expo, axis=-1, keepdims=True)).astype(jnp.bfloat16)
    mixed = jnp.einsum("bhqk,kbhd->qbhd", weights, values, preferred_element_type=jnp.float32)
    return mixed.reshape(packed.shape[:2] + (channels,)).astype(jnp.bfloat16)


def project(flat, weight):
    return jnp.dot(flat, weight, preferred_element_type=jnp.float32).astype(jnp.bfloat16)


def residual_add(base, mixed, weight):
    rows, columns, channels = base.shape
    update = jnp.dot(
        mixed.reshape(rows * columns, channels), weight, preferred_element_type=jnp.float32
    )
    return (base.astype(jnp.float32) + update.reshape(base.shape)).astype(jnp.bfloat16)


def plain(tokens, row_gain, row_qkv, row_out, col_gain, col_qkv, col_out):
    rows, columns, channels = tokens.shape
    normed = normalize(tokens, row_gain).reshape(rows * columns, channels)
    packed = project(normed, row_qkv).reshape(rows, columns, 3 * channels)
    mixed = lax.map(lambda one_row: attend(one_row[:, None, :])[:, 0, :], packed)
    first = residual_add(tokens, mixed, row_out)
    moved = lax.all_to_all(first, AXIS, split_axis=1, concat_axis=0, tiled=True)
    length, count, _ = moved.shape
    flat = normalize(moved, col_gain).reshape(length * count, channels)
    column_mixed = attend(project(flat, col_qkv).reshape(length, count, 3 * channels))
    returned = lax.all_to_all(column_mixed, AXIS, split_axis=0, concat_axis=1, tiled=True)
    return residual_add(first, returned, col_out)


def kernel(
    x_hbm, rg_hbm, rqkv_hbm, rout_hbm, cg_hbm, cqkv_hbm, cout_hbm,
    out_ref,
    rg_ref, cg_ref, x_ref, rqkv_ref, rout_ref, cqkv_ref, cout_ref,
    n_ref, k_ref, v_ref, cv_ref, send_ref, recv_ref, back_ref,
    load_sem, sent_sem, r1_sem, r2_sem,
):
    n, _, channels = x_hbm.shape
    chunks = x_ref.shape[0]
    size = n * TILE
    half = n // 2
    early = min(2, half - 1)
    held = early + half // 4
    head = channels // HEADS
    per = 128 // head
    pairs = channels // 128
    me = lax.axis_index(AXIS)
    mine = me // half
    other = 1 - mine

    loads = [
        pltpu.make_async_copy(
            x_hbm.at[:, pl.ds(c * TILE, TILE), :], x_ref.at[c], load_sem.at[c]
        )
        for c in range(chunks)
    ]
    weights = [
        pltpu.make_async_copy(src, dst, load_sem.at[chunks + i])
        for i, (src, dst) in enumerate(
            [
                (rg_hbm, rg_ref.at[0]),
                (rqkv_hbm, rqkv_ref),
                (rout_hbm, rout_ref),
                (cg_hbm, cg_ref.at[0]),
                (cqkv_hbm, cqkv_ref),
                (cout_hbm, cout_ref),
            ]
        )
    ]
    for copy in weights[:1] + loads + weights[1:3]:
        copy.start()

    barrier = pltpu.get_barrier_semaphore()

    def greet(j, carry):
        peer = lax.rem(me + j, n)
        pl.semaphore_signal(barrier, inc=1, device_id={AXIS: peer}, device_id_type=MESH)
        return carry

    lax.fori_loop(1, n, greet, 0)

    columns = k_ref.shape[0]
    factor = head ** (-0.5) * math.log2(math.e)

    def attention(query, keys, values, mask):
        count = query.shape[0]
        lane = lax.broadcasted_iota(jnp.int32, query.shape, 1) // head
        apart = jnp.concatenate(
            [jnp.where(lane == h, query, jnp.zeros_like(query)) for h in range(per)], axis=0
        )
        scores = lax.dot_general(
            apart, keys, (((1,), (1,)), ((), ())), preferred_element_type=jnp.float32
        )
        if mask is not None:
            scores = jnp.where(mask, scores, -jnp.inf)
        peak = jnp.max(scores, axis=-1, keepdims=True)
        expo = jnp.exp2(scores - peak).astype(jnp.bfloat16)
        both = jnp.dot(expo, values, preferred_element_type=jnp.float32)
        both = both[:, :128] / both[:, 128:]
        mixed = both[:count]
        for h in range(1, per):
            mixed = jnp.where(lane == h, both[h * count : (h + 1) * count], mixed)
        return mixed.astype(jnp.bfloat16)

    for p in range(pairs):
        v_ref[p, :, 128:] = jnp.ones((columns, 128), jnp.bfloat16)
        cv_ref[p, :, 128:] = jnp.ones((size, 128), jnp.bfloat16)
    weights[0].wait()
    for c in range(chunks):
        loads[c].wait()
        normed = normalize(x_ref[c].reshape(size, channels), rg_ref[...])
        n_ref[c] = normed.reshape(n, TILE, channels)
    for copy in weights[3:]:
        copy.start()
    for copy in weights[1:3]:
        copy.wait()
    for c in range(chunks):
        normed = n_ref[c].reshape(size, channels)
        packed = jnp.dot(normed, rqkv_ref[:, channels:], preferred_element_type=jnp.float32)
        k_ref[pl.ds(c * size, size), :] = packed[:, :channels].astype(jnp.bfloat16)
        for p in range(pairs):
            at = channels + p * 128
            v_ref[p, pl.ds(c * size, size), :128] = packed[:, at : at + 128].astype(jnp.bfloat16)

    def copy_out(c, peer):
        return pltpu.make_async_remote_copy(
            src_ref=send_ref.at[c, peer], dst_ref=recv_ref.at[c, me],
            send_sem=sent_sem, recv_sem=r1_sem.at[c],
            device_id={AXIS: peer}, device_id_type=MESH,
        )

    def copies_in(c):
        whole = recv_ref.at[c, pl.ds(0, n - 1)]
        return pltpu.make_async_copy(whole, whole, r1_sem.at[c])

    def back_out(c, peer):
        return pltpu.make_async_remote_copy(
            src_ref=back_ref.at[c, peer], dst_ref=out_ref.at[me, pl.ds(c * TILE, TILE), :],
            send_sem=sent_sem, recv_sem=r2_sem,
            device_id={AXIS: peer}, device_id_type=MESH,
        )

    def across(body, lo=0, hi=half):
        def step(j, carry):
            body(other * half + j)
            return carry

        lax.fori_loop(lo, hi, step, 0)

    def along(body):
        def step(j, carry):
            body(mine * half + lax.rem(me + j, half))
            return carry

        lax.fori_loop(1, half, step, 0)

    def send_back(c, lo, hi):
        def skip(j):
            return mine * half + j + jnp.where(j >= me - mine * half, 1, 0)

        def step(k, carry):
            lower = jnp.where(k < half, k, skip(k - half))
            upper = jnp.where(k < half + early, half + lax.rem((k - early) * (half // 2) + (k - early) // 2, half), skip(k - half))
            upper = jnp.where(k < early, skip(k), upper)
            back_out(c, jnp.where(mine == 1, lower, upper)).start()
            return carry

        lax.fori_loop(lo, hi, step, 0)

    def row_unit(c, start, count):
        at = pl.ds(start, count)
        normed = n_ref[c, at].reshape(count * TILE, channels)
        query = jnp.dot(normed, rqkv_ref[:, :channels], preferred_element_type=jnp.float32)
        query = (query * factor).astype(jnp.bfloat16)
        mixed = jnp.concatenate(
            [
                attention(
                    query[:, p * 128 : (p + 1) * 128],
                    k_ref[:, p * 128 : (p + 1) * 128],
                    v_ref[p],
                    None,
                )
                for p in range(pairs)
            ],
            axis=1,
        )
        update = jnp.dot(mixed, rout_ref[...], preferred_element_type=jnp.float32)
        base = x_ref[c, at].reshape(count * TILE, channels).astype(jnp.float32)
        first = (base + update).astype(jnp.bfloat16)
        send_ref[c, at] = first.reshape(count, TILE, channels)

    def row_across(c, splits=1):
        count = half // splits
        for i in range(splits):
            row_unit(c, other * half + i * count, count)
            if i == 0 and splits > 1:
                pl.semaphore_wait(barrier, n - 1)
            across(lambda peer: copy_out(c, peer).start(), i * count, (i + 1) * count)

    def row_along(c):
        row_unit(c, mine * half, half)
        along(lambda peer: copy_out(c, peer).start())
        recv_ref[c, me] = send_ref[c, me]

    def row_step(c, carry):
        row_across(c)
        row_along(c - 1)
        return carry

    row_across(0, 2)
    lax.fori_loop(1, chunks, row_step, 0)
    row_along(chunks - 1)
    for copy in weights[3:]:
        copy.wait()

    at_row = lax.broadcasted_iota(jnp.int32, (per * size, size), 0)
    at_col = lax.broadcasted_iota(jnp.int32, (per * size, size), 1)
    same = lax.rem(at_row, TILE) == lax.rem(at_col, TILE)

    def col_chunk(c, carry):
        copies_in(c).wait()
        base = recv_ref[c].reshape(size, channels)
        normed = normalize(base, cg_ref[...])
        packed = jnp.dot(normed, cqkv_ref[...], preferred_element_type=jnp.float32)
        query = (packed[:, :channels] * factor).astype(jnp.bfloat16)
        keys = packed[:, channels : 2 * channels].astype(jnp.bfloat16)
        for p in range(pairs):
            at = 2 * channels + p * 128
            cv_ref[p, :, :128] = packed[:, at : at + 128].astype(jnp.bfloat16)
        mixed = jnp.concatenate(
            [
                attention(
                    query[:, p * 128 : (p + 1) * 128],
                    keys[:, p * 128 : (p + 1) * 128],
                    cv_ref[p],
                    same,
                )
                for p in range(pairs)
            ],
            axis=1,
        )
        update = jnp.dot(mixed, cout_ref[...], preferred_element_type=jnp.float32)
        result = (base.astype(jnp.float32) + update).astype(jnp.bfloat16)
        back_ref[c] = result.reshape(n, TILE, channels)

        ready = jnp.where((c < chunks - 2) | (mine == 0), n - 1, held)
        send_back(c, 0, jnp.where(c == chunks - 1, early, ready))

        out_ref[me, pl.ds(c * TILE, TILE), :] = back_ref[c, me]
        return carry

    lax.fori_loop(0, chunks, col_chunk, 0)
    if chunks > 1:
        send_back(chunks - 2, jnp.where(mine == 0, n - 1, held), n - 1)
    send_back(chunks - 1, early, n - 1)

    out_part = out_ref.at[pl.ds(0, n - 1)]
    send_part = send_ref.at[:, pl.ds(0, n - 1)]
    back_part = back_ref.at[:, pl.ds(0, n - 1)]
    pltpu.make_async_copy(send_part, send_part, sent_sem).wait()
    pltpu.make_async_copy(back_part, back_part, sent_sem).wait()
    pltpu.make_async_copy(out_part, out_part, r2_sem).wait()


def fused(n, tokens, row_gain, row_qkv, row_out, col_gain, col_qkv, col_out):
    _, columns, channels = tokens.shape
    chunks = columns // (n * TILE)
    size = n * TILE
    pairs = channels // 128
    bf16 = jnp.bfloat16
    hbm = pl.BlockSpec(memory_space=pl.ANY)
    dma = pltpu.SemaphoreType.DMA
    flops = 2 * columns * channels * (8 * channels + 2 * columns + 2 * size)
    out = pl.pallas_call(
        kernel,
        out_shape=pltpu.VMEM((n, columns // n, channels), bf16),
        in_specs=[hbm] * 7,
        out_specs=pl.BlockSpec(memory_space=pltpu.VMEM),
        scratch_shapes=[
            pltpu.VMEM((1, channels), jnp.float32),
            pltpu.VMEM((1, channels), jnp.float32),
            pltpu.VMEM((chunks, n, TILE, channels), bf16),
            pltpu.VMEM((channels, 3 * channels), bf16),
            pltpu.VMEM((channels, channels), bf16),
            pltpu.VMEM((channels, 3 * channels), bf16),
            pltpu.VMEM((channels, channels), bf16),
            pltpu.VMEM((chunks, n, TILE, channels), bf16),
            pltpu.VMEM((columns, channels), bf16),
            pltpu.VMEM((pairs, columns, 256), bf16),
            pltpu.VMEM((pairs, size, 256), bf16),
            pltpu.VMEM((chunks, n, TILE, channels), bf16),
            pltpu.VMEM((chunks, n, TILE, channels), bf16),
            pltpu.VMEM((chunks, n, TILE, channels), bf16),
            dma((chunks + 6,)),
            dma(()),
            dma((chunks,)),
            dma(()),
        ],
        compiler_params=pltpu.CompilerParams(
            collective_id=0, has_side_effects=True, vmem_limit_bytes=60000000
        ),
        cost_estimate=pl.CostEstimate(
            flops=flops, bytes_accessed=8 * columns * channels, transcendentals=0
        ),
    )(
        tokens.reshape(n, columns // n, channels),
        row_gain,
        row_qkv,
        row_out,
        col_gain,
        col_qkv,
        col_out,
    )
    return out.reshape(tokens.shape)


def solution(mesh):
    n = mesh.shape[AXIS]

    def body(tokens, *rest):
        rows, columns, channels = tokens.shape
        whole_tiles = rows == 1 and columns % (n * TILE) == 0 and channels % 128 == 0
        if n % 4 == 0 and whole_tiles and 128 % (channels // HEADS) == 0:
            return fused(n, tokens, *rest)
        return plain(tokens, *rest)

    in_specs = (P(("grp", AXIS), None, None), P(), P(), P(), P(), P(), P())
    out_specs = P(("grp", AXIS), None, None)
    return jax.shard_map(body, mesh=mesh, in_specs=in_specs, out_specs=out_specs, check_vma=False)
```

```python
import functools
import math

import jax
import jax.numpy as jnp
from jax import lax
from jax.experimental import pallas as pl
from jax.experimental.pallas import tpu as pltpu
from jax.sharding import PartitionSpec as P

HEADS = 6
AXIS = "wide"
TILE = 16
MESH = pl.DeviceIdType.MESH


def normalize(values, gain):
    floats = values.astype(jnp.float32)
    scale = lax.rsqrt(jnp.mean(floats * floats, axis=-1, keepdims=True) + 1e-06)
    return (floats * scale * gain).astype(jnp.bfloat16)


def attend(packed):
    channels = packed.shape[-1] // 3
    head_size = channels // HEADS
    shape = packed.shape[:2] + (HEADS, head_size)
    query = packed[..., :channels].reshape(shape)
    keys = packed[..., channels : 2 * channels].reshape(shape)
    values = packed[..., 2 * channels :].reshape(shape)
    scores = jnp.einsum(
        "qbhd,kbhd->bhqk", query, keys, preferred_element_type=jnp.float32
    ) * head_size ** (-0.5)
    scores = scores - jnp.max(scores, axis=-1, keepdims=True)
    expo = jnp.exp(scores)
    weights = (expo / jnp.sum(expo, axis=-1, keepdims=True)).astype(jnp.bfloat16)
    mixed = jnp.einsum("bhqk,kbhd->qbhd", weights, values, preferred_element_type=jnp.float32)
    return mixed.reshape(packed.shape[:2] + (channels,)).astype(jnp.bfloat16)


def project(flat, weight):
    return jnp.dot(flat, weight, preferred_element_type=jnp.float32).astype(jnp.bfloat16)


def residual_add(base, mixed, weight):
    rows, columns, channels = base.shape
    update = jnp.dot(
        mixed.reshape(rows * columns, channels), weight, preferred_element_type=jnp.float32
    )
    return (base.astype(jnp.float32) + update.reshape(base.shape)).astype(jnp.bfloat16)


def plain(tokens, row_gain, row_qkv, row_out, col_gain, col_qkv, col_out):
    rows, columns, channels = tokens.shape
    normed = normalize(tokens, row_gain).reshape(rows * columns, channels)
    packed = project(normed, row_qkv).reshape(rows, columns, 3 * channels)
    mixed = lax.map(lambda one_row: attend(one_row[:, None, :])[:, 0, :], packed)
    first = residual_add(tokens, mixed, row_out)
    moved = lax.all_to_all(first, AXIS, split_axis=1, concat_axis=0, tiled=True)
    length, count, _ = moved.shape
    flat = normalize(moved, col_gain).reshape(length * count, channels)
    column_mixed = attend(project(flat, col_qkv).reshape(length, count, 3 * channels))
    returned = lax.all_to_all(column_mixed, AXIS, split_axis=0, concat_axis=1, tiled=True)
    return residual_add(first, returned, col_out)


def kernel(
    x_hbm, rg_hbm, rqkv_hbm, rout_hbm, cg_hbm, cqkv_hbm, cout_hbm,
    out_ref,
    rg_ref, cg_ref, x_ref, rqkv_ref, rout_ref, cqkv_ref, cout_ref,
    n_ref, k_ref, v_ref, cv_ref, send_ref, recv_ref, back_ref,
    load_sem, sent_sem, r1_sem, r2_sem,
):
    n, _, channels = x_hbm.shape
    chunks = x_ref.shape[0]
    size = n * TILE
    half = n // 2
    early = min(2, half - 1)
    held = early + half // 4
    head = channels // HEADS
    per = 128 // head
    pairs = channels // 128
    me = lax.axis_index(AXIS)
    mine = me // half
    other = 1 - mine

    loads = [
        pltpu.make_async_copy(
            x_hbm.at[:, pl.ds(c * TILE, TILE), :], x_ref.at[c], load_sem.at[c]
        )
        for c in range(chunks)
    ]
    weights = [
        pltpu.make_async_copy(src, dst, load_sem.at[chunks + i])
        for i, (src, dst) in enumerate(
            [
                (rg_hbm, rg_ref.at[0]),
                (rqkv_hbm, rqkv_ref),
                (rout_hbm, rout_ref),
                (cg_hbm, cg_ref.at[0]),
                (cqkv_hbm, cqkv_ref),
                (cout_hbm, cout_ref),
            ]
        )
    ]
    for copy in weights[:1] + loads + weights[1:3]:
        copy.start()

    barrier = pltpu.get_barrier_semaphore()

    def greet(j, carry):
        peer = lax.rem(me + j, n)
        pl.semaphore_signal(barrier, inc=1, device_id={AXIS: peer}, device_id_type=MESH)
        return carry

    lax.fori_loop(1, n, greet, 0)

    columns = k_ref.shape[0]
    factor = head ** (-0.5) * math.log2(math.e)

    def attention(query, keys, values, mask):
        count = query.shape[0]
        lane = lax.broadcasted_iota(jnp.int32, query.shape, 1) // head
        apart = jnp.concatenate(
            [jnp.where(lane == h, query, jnp.zeros_like(query)) for h in range(per)], axis=0
        )
        scores = lax.dot_general(
            apart, keys, (((1,), (1,)), ((), ())), preferred_element_type=jnp.float32
        )
        if mask is not None:
            scores = jnp.where(mask, scores, -jnp.inf)
        peak = jnp.max(scores, axis=-1, keepdims=True)
        expo = jnp.exp2(scores - peak).astype(jnp.bfloat16)
        both = jnp.dot(expo, values, preferred_element_type=jnp.float32)
        both = both[:, :128] / both[:, 128:]
        mixed = both[:count]
        for h in range(1, per):
            mixed = jnp.where(lane == h, both[h * count : (h + 1) * count], mixed)
        return mixed.astype(jnp.bfloat16)

    for p in range(pairs):
        v_ref[p, :, 128:] = jnp.ones((columns, 128), jnp.bfloat16)
        cv_ref[p, :, 128:] = jnp.ones((size, 128), jnp.bfloat16)
    weights[0].wait()
    for c in range(chunks):
        loads[c].wait()
        normed = normalize(x_ref[c].reshape(size, channels), rg_ref[...])
        n_ref[c] = normed.reshape(n, TILE, channels)
    for copy in weights[3:]:
        copy.start()
    for copy in weights[1:3]:
        copy.wait()
    for c in range(chunks):
        normed = n_ref[c].reshape(size, channels)
        packed = jnp.dot(normed, rqkv_ref[:, channels:], preferred_element_type=jnp.float32)
        k_ref[pl.ds(c * size, size), :] = packed[:, :channels].astype(jnp.bfloat16)
        for p in range(pairs):
            at = channels + p * 128
            v_ref[p, pl.ds(c * size, size), :128] = packed[:, at : at + 128].astype(jnp.bfloat16)

    def copy_out(c, peer):
        return pltpu.make_async_remote_copy(
            src_ref=send_ref.at[c, peer], dst_ref=recv_ref.at[c, me],
            send_sem=sent_sem, recv_sem=r1_sem.at[c],
            device_id={AXIS: peer}, device_id_type=MESH,
        )

    def copies_in(c):
        whole = recv_ref.at[c, pl.ds(0, n - 1)]
        return pltpu.make_async_copy(whole, whole, r1_sem.at[c])

    def back_out(c, peer):
        return pltpu.make_async_remote_copy(
            src_ref=back_ref.at[c, peer], dst_ref=out_ref.at[me, pl.ds(c * TILE, TILE), :],
            send_sem=sent_sem, recv_sem=r2_sem,
            device_id={AXIS: peer}, device_id_type=MESH,
        )

    def across(body, lo=0, hi=half):
        def step(j, carry):
            body(other * half + j)
            return carry

        lax.fori_loop(lo, hi, step, 0)

    def along(body):
        def step(j, carry):
            body(mine * half + lax.rem(me + j, half))
            return carry

        lax.fori_loop(1, half, step, 0)

    def send_back(c, lo, hi):
        def skip(j):
            return mine * half + j + jnp.where(j >= me - mine * half, 1, 0)

        def step(k, carry):
            lower = jnp.where(k < half, k, skip(k - half))
            upper = jnp.where(k < half + early, half + lax.rem((k - early) * (half // 2) + (k - early) // 2, half), skip(k - half))
            upper = jnp.where(k < early, skip(k), upper)
            back_out(c, jnp.where(mine == 1, lower, upper)).start()
            return carry

        lax.fori_loop(lo, hi, step, 0)

    def row_unit(c, start, count):
        at = pl.ds(start, count)
        normed = n_ref[c, at].reshape(count * TILE, channels)
        query = jnp.dot(normed, rqkv_ref[:, :channels], preferred_element_type=jnp.float32)
        query = (query * factor).astype(jnp.bfloat16)
        mixed = jnp.concatenate(
            [
                attention(
                    query[:, p * 128 : (p + 1) * 128],
                    k_ref[:, p * 128 : (p + 1) * 128],
                    v_ref[p],
                    None,
                )
                for p in range(pairs)
            ],
            axis=1,
        )
        update = jnp.dot(mixed, rout_ref[...], preferred_element_type=jnp.float32)
        base = x_ref[c, at].reshape(count * TILE, channels).astype(jnp.float32)
        first = (base + update).astype(jnp.bfloat16)
        send_ref[c, at] = first.reshape(count, TILE, channels)

    def row_across(c, splits=1):
        count = half // splits
        for i in range(splits):
            row_unit(c, other * half + i * count, count)
            if i == 0 and splits > 1:
                pl.semaphore_wait(barrier, n - 1)
            across(lambda peer: copy_out(c, peer).start(), i * count, (i + 1) * count)

    def row_along(c):
        row_unit(c, mine * half, half)
        along(lambda peer: copy_out(c, peer).start())
        recv_ref[c, me] = send_ref[c, me]

    def row_step(c, carry):
        row_across(c)
        return carry

    def row_rest(c, carry):
        row_along(c)
        return carry

    row_across(0, 2)
    lax.fori_loop(1, chunks, row_step, 0)
    lax.fori_loop(0, chunks, row_rest, 0)
    for copy in weights[3:]:
        copy.wait()

    at_row = lax.broadcasted_iota(jnp.int32, (per * size, size), 0)
    at_col = lax.broadcasted_iota(jnp.int32, (per * size, size), 1)
    same = lax.rem(at_row, TILE) == lax.rem(at_col, TILE)

    def col_chunk(c, carry):
        copies_in(c).wait()
        base = recv_ref[c].reshape(size, channels)
        normed = normalize(base, cg_ref[...])
        packed = jnp.dot(normed, cqkv_ref[...], preferred_element_type=jnp.float32)
        query = (packed[:, :channels] * factor).astype(jnp.bfloat16)
        keys = packed[:, channels : 2 * channels].astype(jnp.bfloat16)
        for p in range(pairs):
            at = 2 * channels + p * 128
            cv_ref[p, :, :128] = packed[:, at : at + 128].astype(jnp.bfloat16)
        mixed = jnp.concatenate(
            [
                attention(
                    query[:, p * 128 : (p + 1) * 128],
                    keys[:, p * 128 : (p + 1) * 128],
                    cv_ref[p],
                    same,
                )
                for p in range(pairs)
            ],
            axis=1,
        )
        update = jnp.dot(mixed, cout_ref[...], preferred_element_type=jnp.float32)
        result = (base.astype(jnp.float32) + update).astype(jnp.bfloat16)
        back_ref[c] = result.reshape(n, TILE, channels)

        ready = jnp.where((c < chunks - 2) | (mine == 0), n - 1, held)
        send_back(c, 0, jnp.where(c == chunks - 1, early, ready))

        out_ref[me, pl.ds(c * TILE, TILE), :] = back_ref[c, me]
        return carry

    lax.fori_loop(0, chunks, col_chunk, 0)
    if chunks > 1:
        send_back(chunks - 2, jnp.where(mine == 0, n - 1, held), n - 1)
    send_back(chunks - 1, early, n - 1)

    out_part = out_ref.at[pl.ds(0, n - 1)]
    send_part = send_ref.at[:, pl.ds(0, n - 1)]
    back_part = back_ref.at[:, pl.ds(0, n - 1)]
    pltpu.make_async_copy(send_part, send_part, sent_sem).wait()
    pltpu.make_async_copy(back_part, back_part, sent_sem).wait()
    pltpu.make_async_copy(out_part, out_part, r2_sem).wait()


def fused(n, tokens, row_gain, row_qkv, row_out, col_gain, col_qkv, col_out):
    _, columns, channels = tokens.shape
    chunks = columns // (n * TILE)
    size = n * TILE
    pairs = channels // 128
    bf16 = jnp.bfloat16
    hbm = pl.BlockSpec(memory_space=pl.ANY)
    dma = pltpu.SemaphoreType.DMA
    flops = 2 * columns * channels * (8 * channels + 2 * columns + 2 * size)
    out = pl.pallas_call(
        kernel,
        out_shape=pltpu.VMEM((n, columns // n, channels), bf16),
        in_specs=[hbm] * 7,
        out_specs=pl.BlockSpec(memory_space=pltpu.VMEM),
        scratch_shapes=[
            pltpu.VMEM((1, channels), jnp.float32),
            pltpu.VMEM((1, channels), jnp.float32),
            pltpu.VMEM((chunks, n, TILE, channels), bf16),
            pltpu.VMEM((channels, 3 * channels), bf16),
            pltpu.VMEM((channels, channels), bf16),
            pltpu.VMEM((channels, 3 * channels), bf16),
            pltpu.VMEM((channels, channels), bf16),
            pltpu.VMEM((chunks, n, TILE, channels), bf16),
            pltpu.VMEM((columns, channels), bf16),
            pltpu.VMEM((pairs, columns, 256), bf16),
            pltpu.VMEM((pairs, size, 256), bf16),
            pltpu.VMEM((chunks, n, TILE, channels), bf16),
            pltpu.VMEM((chunks, n, TILE, channels), bf16),
            pltpu.VMEM((chunks, n, TILE, channels), bf16),
            dma((chunks + 6,)),
            dma(()),
            dma((chunks,)),
            dma(()),
        ],
        compiler_params=pltpu.CompilerParams(
            collective_id=0, has_side_effects=True, vmem_limit_bytes=60000000
        ),
        cost_estimate=pl.CostEstimate(
            flops=flops, bytes_accessed=8 * columns * channels, transcendentals=0
        ),
    )(
        tokens.reshape(n, columns // n, channels),
        row_gain,
        row_qkv,
        row_out,
        col_gain,
        col_qkv,
        col_out,
    )
    return out.reshape(tokens.shape)


def solution(mesh):
    n = mesh.shape[AXIS]

    def body(tokens, *rest):
        rows, columns, channels = tokens.shape
        whole_tiles = rows == 1 and columns % (n * TILE) == 0 and channels % 128 == 0
        if n % 4 == 0 and whole_tiles and 128 % (channels // HEADS) == 0:
            return fused(n, tokens, *rest)
        return plain(tokens, *rest)

    in_specs = (P(("grp", AXIS), None, None), P(), P(), P(), P(), P(), P())
    out_specs = P(("grp", AXIS), None, None)
    return jax.shard_map(body, mesh=mesh, in_specs=in_specs, out_specs=out_specs, check_vma=False)
```
